256 devices in a mesh: row: 16 (over z, core), col: 4 (over y), layer: 4 (over x).
Axes of the slice: x: 4, y: 4, z: 8, core: 2. Of those that a mesh axis runs over, the one named last changes fastest.
Arguments:
- left_mant: bfloat16 [3, 5, 6, 1024, 4, 256], P(None, None, None, ('row', 'col'), 'layer'), may hold values from 9.983778e-07 to 1
- right_mant: bfloat16 [3, 5, 6, 4, 256, 1024], P(None, None, None, 'layer', 'row', 'col'), may hold values from 9.983778e-07 to 1
- left_scale: float32 [3, 5], replicated, may hold values from -750 to 0
- right_scale: float32 [3, 5], replicated, may hold values from -750 to 0
- rule_probs: float32 [6, 6, 6], replicated, may hold values from 0.05 to 1
- pair_logp: float32 [6, 4, 4], replicated, may hold values from -4 to 4
- nucleotides: int32 [65536], replicated, may hold values from 0 to 3
- first_block: int32 [1], replicated, may hold values from 0 to 55
Outputs:
- block_values: float32 [3, 6, 1024, 1024], P(None, None, ('row', 'layer'), 'col')
- block_scale: float32 [3], replicated
The draws below stay inside these ranges and needn't reach their ends.
All inputs are finite; a program needn't handle non-finite values.
Results may differ from the reference program's by a relative error of at most 0.0003.
Values may be sent and summed in bfloat16 or wider, within the bound.
No kernel may reach another device: no remote copies, remote signals or barrier semaphores. Data moves between devices by JAX's collectives and lax.ppermute only.
A program may use at most 64 MiB of HBM per device.

```python
import math
import jax
import jax.numpy as jnp
from jax import lax

NT = 6
BLK = 1024
SPLITS = 5
NOUT = 3
LENGTH = 65536
KGROUPS = 4
KWIDTH = 256


def scale_levels(key):
    stepping = jax.random.uniform(jax.random.fold_in(key, 11), (NOUT + SPLITS + 1,), jnp.float32, -150.0, -60.0)
    return jnp.concatenate([jnp.zeros((1,), jnp.float32), jnp.cumsum(stepping)])


def scale_jitter(key, salt):
    return jax.random.uniform(jax.random.fold_in(key, salt), (NOUT, SPLITS), jnp.float32, 0.0, 1.5)


def draw_left_scale(key, part):
    levels = scale_levels(key)
    starts = jnp.arange(NOUT)[:, None]
    reaches = jnp.arange(1, SPLITS + 1)[None, :]
    return levels[starts + reaches] - levels[starts] + scale_jitter(key, 23)


def draw_right_scale(key, part):
    levels = scale_levels(key)
    starts = jnp.arange(NOUT)[:, None]
    reaches = jnp.arange(1, SPLITS + 1)[None, :]
    return levels[starts + SPLITS + 1] - levels[starts + reaches] + scale_jitter(key, 37)


def with_ends(drawn, stream_key, low, largest):
    spot = [jax.random.randint(jax.random.fold_in(stream_key, axis), (), 0, length) for axis, length in enumerate(drawn.shape)]
    main_axis = drawn.shape.index(max(drawn.shape))
    beside = spot[:main_axis] + [(spot[main_axis] + 1) % drawn.shape[main_axis]] + spot[main_axis + 1:]
    return drawn.at[tuple(spot)].set(low).at[tuple(beside)].set(largest)


def block_levels(key, extent, cuts, smallest, top_value):
    factor_of, own = 1.0, jax.random.fold_in(key, 6)
    for dim, shards_of in cuts:
        draws = jnp.exp(jax.random.uniform(jax.random.fold_in(own, dim), (shards_of,), jnp.float32, smallest / len(cuts), top_value / len(cuts)))
        factor_of = factor_of * jnp.repeat(draws, extent[dim] // shards_of).reshape([-1 if axis == dim else 1 for axis in range(len(extent))])
    return factor_of


def centred(key, dims, width, limit, dtype=jnp.bfloat16):
    drawn = jax.random.normal(key, dims, jnp.float32) * width
    return jnp.minimum(jnp.maximum(drawn, -limit), limit).astype(dtype)


def setup_inputs(seed: int = 0) -> dict:
    key_of = jax.random.split(jax.random.key(seed), 9)
    return {
        "left_mant": jnp.clip(jnp.exp(math.log(1.0) - 13.817134 * jax.random.uniform(key_of[0], (NOUT, SPLITS, NT, BLK, KGROUPS, KWIDTH), jnp.float32) ** block_levels(key_of[0], (NOUT, SPLITS, NT, BLK, KGROUPS, KWIDTH), ((3, 64), (4, 4)), -0.2, 0.2)), 9.98377799987793e-07, 1.0).astype(jnp.bfloat16),
        "right_mant": jnp.clip(jnp.exp(math.log(1.0) - 13.817134 * jax.random.uniform(key_of[1], (NOUT, SPLITS, NT, KGROUPS, KWIDTH, BLK), jnp.float32) ** block_levels(key_of[1], (NOUT, SPLITS, NT, KGROUPS, KWIDTH, BLK), ((3, 4), (4, 16), (5, 4)), -0.2, 0.2)), 9.98377799987793e-07, 1.0).astype(jnp.bfloat16),
        "left_scale": draw_left_scale(jax.random.fold_in(key_of[8], 71), 0),
        "right_scale": draw_right_scale(jax.random.fold_in(key_of[8], 71), 0),
        "rule_probs": jnp.clip(jnp.exp(jax.random.uniform(key_of[4], (NT, NT, NT), jnp.float32, math.log(0.05), math.log(1.0))), 0.05, 1.0),
        "pair_logp": centred(key_of[5], (NT, 4, 4), 1.0, 4.0, jnp.float32),
        "nucleotides": with_ends(jax.random.randint(key_of[6], (LENGTH,), 0, 4), jax.random.fold_in(key_of[6], 1), 0, 3).astype(jnp.int32),
        "first_block": jax.random.randint(key_of[7], (1,), 0, LENGTH // BLK - NOUT - SPLITS).astype(jnp.int32),
    }


def reference(left_mant, right_mant, left_scale, right_scale, rule_probs, pair_logp, nucleotides, first_block):
    total_scale = left_scale + right_scale
    highest = jnp.max(total_scale, axis=1)
    weight = jnp.exp(total_scale - highest[:, None])
    mixing = (rule_probs[None, None] * weight[:, :, None, None, None]).astype(jnp.bfloat16)
    inside_list = []
    for block_id in range(NOUT):
        summed = jnp.zeros((NT, BLK, BLK), jnp.float32)
        for split_id in range(SPLITS):
            left_block = left_mant[block_id, split_id].reshape(NT, BLK, BLK)
            right_block = right_mant[block_id, split_id].reshape(NT, BLK, BLK)
            mixed_part = jnp.einsum("xyz,yik->xzik", mixing[block_id, split_id].astype(jnp.float32), left_block.astype(jnp.float32), precision=lax.Precision.HIGHEST).astype(jnp.bfloat16)
            summed = summed + jnp.einsum("xzik,zkj->xij", mixed_part.astype(jnp.float32), right_block.astype(jnp.float32), precision=lax.Precision.HIGHEST)
        row_start = ((first_block[0] + block_id) * BLK).astype(jnp.int32)
        col_start = ((first_block[0] + block_id + SPLITS + 1) * BLK).astype(jnp.int32)
        row_codes = lax.dynamic_slice_in_dim(nucleotides, row_start, BLK)
        col_codes = lax.dynamic_slice_in_dim(nucleotides, col_start, BLK)
        pairing = pair_logp[:, row_codes[:, None], col_codes[None, :]]
        inside_list.append(highest[block_id] + jnp.log(summed) + pairing)
    inside = jnp.stack(inside_list)
    peak_value = jnp.max(inside, axis=(1, 2, 3))
    return inside - peak_value[:, None, None, None], peak_value
```

```python
import functools

import jax
import jax.numpy as jnp
from jax import lax
from jax.experimental import pallas as pl
from jax.experimental.pallas import tpu as pltpu
from jax.sharding import Mesh
from jax.sharding import PartitionSpec as P


ZC = ("z", "core")
OWNER = (0, 1, 0)
F32 = jnp.float32
BF16 = jnp.bfloat16


def shift(count, by):
    return [(i, (i + by) % count) for i in range(count)]


SWAP = [(0, 1), (1, 0)]


def ring_pairs(nz, cores=(0, 1)):
    pairs = []
    for z in range(nz):
        if 0 in cores:
            pairs.append((2 * z, 2 * ((z + 1) % nz)))
        if 1 in cores:
            pairs.append((2 * z + 1, 2 * ((z - 1) % nz) + 1))
    return pairs


def wanted_positions(z, who, owner, column, nz, width):
    piece, within = column // width, column % width
    step = jnp.where(who == 0, -1, 1) * (piece + 1)
    last = jnp.where(who == owner, 0, nz // 2)
    block = (z + jnp.where(piece == 3, last, step) + 2 * nz) % nz
    return block * width + within


def pick_kernel(nz, ids_ref, left_ref, keep_ref, send_ref):
    z, core = ids_ref[0], ids_ref[1]
    owner = jnp.where(pl.program_id(0) == 1, OWNER[1], OWNER[0])
    depth = left_ref.shape[2]
    half = depth // 2
    row = lax.broadcasted_iota(jnp.int32, (depth, half), 0)
    column = lax.broadcasted_iota(jnp.int32, (depth, half), 1)
    for who, out in ((core, keep_ref), (1 - core, send_ref)):
        source = wanted_positions(z, who, owner, column, nz, half // 4)
        chosen = jnp.where(row == source, 1.0, 0.0).astype(BF16)
        out[0] = jnp.dot(left_ref[0], chosen, preferred_element_type=F32).astype(BF16)


def pick(ids, left, nz):
    b, rows, depth = left.shape
    out = jax.ShapeDtypeStruct((b, rows, depth // 2), BF16)
    block = pl.BlockSpec((1, rows, depth // 2), lambda i, ids: (i, 0, 0))
    return pl.pallas_call(
        functools.partial(pick_kernel, nz),
        out_shape=(out, out),
        grid_spec=pltpu.PrefetchScalarGridSpec(
            num_scalar_prefetch=1,
            grid=(b,),
            in_specs=[pl.BlockSpec((1, rows, depth), lambda i, ids: (i, 0, 0))],
            out_specs=(block, block),
        ),
        name="pick",
    )(ids, left)


def mix_kernel(nt, kron_ref, *refs):
    mine, theirs, out_ref = refs[:4], refs[4:8], refs[8]
    kron = kron_ref[0, 0]
    for d in range(4):
        rhs = jnp.concatenate([mine[d][0], theirs[d][0]], axis=1)
        o = jnp.dot(kron, rhs, preferred_element_type=F32).astype(BF16)
        for x in range(nt):
            for z in range(nt):
                top = (x * nt + z) * 16
                for r in range(2):
                    at = x * 128 + r * 64 + d * 16
                    out_ref[0, at : at + 16, z * 128 : (z + 1) * 128] = o[top : top + 16, r * 128 : (r + 1) * 128]


def mix(b, kron, mine, theirs, nt):
    splits = kron.shape[1]
    rows = nt * 16
    piece = pl.BlockSpec((1, rows, 128), lambda s: (b, s, 0))
    return pl.pallas_call(
        functools.partial(mix_kernel, nt),
        out_shape=jax.ShapeDtypeStruct((splits, nt * 128, nt * 128), BF16),
        grid=(splits,),
        in_specs=[pl.BlockSpec((1, 1, nt * rows, rows), lambda s: (b, s, 0, 0))] + [piece] * 8,
        out_specs=pl.BlockSpec((1, nt * 128, nt * 128), lambda s: (s, 0, 0)),
        name=f"mix{b}",
    )(kron, *mine, *theirs)


def contract_kernel(nt, owner, ids_ref, mixed_ref, p1, p2, p3, own, far, keep_ref, send_ref, acc):
    s = pl.program_id(0)
    last = jnp.where(ids_ref[1] == owner, own[0], far[0])
    rhs = jnp.concatenate([p1[0], p2[0], p3[0], last], axis=1)
    rhs = rhs.reshape(rhs.shape[0] * rhs.shape[1], rhs.shape[2])
    part = jnp.dot(mixed_ref[0], rhs, preferred_element_type=F32)

    @pl.when(s == 0)
    def _():
        acc[...] = part

    @pl.when(s > 0)
    def _():
        acc[...] += part

    @pl.when(s == pl.num_programs(0) - 1)
    def _():
        for x in range(nt):
            for d in range(4):
                keep_ref[x, d] = acc[x * 128 + d * 16 : x * 128 + d * 16 + 16, :]
                send_ref[x, d] = acc[x * 128 + 64 + d * 16 : x * 128 + 64 + d * 16 + 16, :]


def contract(b, ids, mixed, pieces, own, far, nt):
    splits, wide = mixed.shape[0], mixed.shape[1]
    cols = own.shape[3]
    piece = pl.BlockSpec((1,) + own.shape[1:], lambda s, ids: (s, 0, 0, 0))
    out = jax.ShapeDtypeStruct((nt, 4, 16, cols), F32)
    whole = pl.BlockSpec((nt, 4, 16, cols), lambda s, ids: (0, 0, 0, 0))
    return pl.pallas_call(
        functools.partial(contract_kernel, nt, OWNER[b]),
        out_shape=(out, out),
        grid_spec=pltpu.PrefetchScalarGridSpec(
            num_scalar_prefetch=1,
            grid=(splits,),
            in_specs=[pl.BlockSpec((1, wide, wide), lambda s, ids: (s, 0, 0))] + [piece] * 5,
            out_specs=(whole, whole),
            scratch_shapes=[pltpu.VMEM((wide, cols), F32)],
        ),
        name=f"contract{b}",
    )(ids, mixed, *pieces, own, far)


def add_kernel(ids_ref, keep_ref, got_ref, *outs):
    y, x = ids_ref[2], ids_ref[3]
    for d, out in enumerate(outs):
        at = (x + d - y + 4) % 4
        out[...] = keep_ref[:, at] + got_ref[:, at]


def add_cores(b, ids, keep, got):
    nt, n, rows, cols = keep.shape
    out = jax.ShapeDtypeStruct((nt, rows, cols), F32)
    whole = pl.BlockSpec((nt, n, rows, cols), lambda i, ids: (0, 0, 0, 0))
    piece = pl.BlockSpec((nt, rows, cols), lambda i, ids: (0, 0, 0))
    return pl.pallas_call(
        add_kernel,
        out_shape=(out,) * 4,
        grid_spec=pltpu.PrefetchScalarGridSpec(
            num_scalar_prefetch=1, grid=(1,), in_specs=[whole, whole], out_specs=(piece,) * 4
        ),
        name=f"add{b}",
    )(ids, keep, got)


def finish_kernel(b, ids_ref, pair_ref, high_ref, row_ref, col_ref, t0, t1, t2, t3, out_ref, max_ref):
    z, core, y, x = ids_ref[0], ids_ref[1], ids_ref[2], ids_ref[3]
    nt, rows, cols = out_ref.shape
    start = ((z * 2 + core) * 4 + x) * rows
    line = row_ref[pl.ds(start // 128, 1), :].astype(F32)
    lane = lax.broadcasted_iota(jnp.int32, (rows, 128), 1)
    sub = lax.broadcasted_iota(jnp.int32, (rows, 128), 0)
    code = jnp.sum(jnp.where(lane == start % 128 + sub, line, 0.0), axis=1, keepdims=True)
    first = y * (cols // 128)
    column = jnp.concatenate([col_ref[pl.ds(first + n, 1), :] for n in range(cols // 128)], axis=1)
    high = high_ref[b]
    best = None
    for n in range(nt):
        def factor(u):
            base = (n * 4 + u) * 4
            t = jnp.where(column == 0, pair_ref[base], pair_ref[base + 1])
            t = jnp.where(column == 2, pair_ref[base + 2], t)
            return jnp.where(column == 3, pair_ref[base + 3], t)

        pairing = jnp.where(code == 0.0, factor(0), factor(1))
        pairing = jnp.where(code == 2.0, factor(2), pairing)
        pairing = jnp.where(code == 3.0, factor(3), pairing)
        summed = (t0[n] + t1[n]) + (t2[n] + t3[n])
        inside = high + jnp.log(summed) + pairing
        out_ref[n] = inside
        best = inside if best is None else jnp.maximum(best, inside)
    best = jnp.max(best, axis=1, keepdims=True)
    best = jnp.max(best, axis=0, keepdims=True)
    max_ref[...] = jnp.broadcast_to(best, max_ref.shape)


def finish(b, ids, pair, high, codes, parts, splits):
    nt, rows, cols = parts[0].shape
    piece = pl.BlockSpec((nt, rows, cols), lambda i, ids, pair, high: (0, 0, 0))
    return pl.pallas_call(
        functools.partial(finish_kernel, b),
        out_shape=(jax.ShapeDtypeStruct((nt, rows, cols), F32), jax.ShapeDtypeStruct((8, 128), F32)),
        grid_spec=pltpu.PrefetchScalarGridSpec(
            num_scalar_prefetch=3,
            grid=(1,),
            in_specs=[
                pl.BlockSpec((8, 128), lambda i, ids, pair, high: (ids[4] + b, 0)),
                pl.BlockSpec((8, 128), lambda i, ids, pair, high: (ids[4] + b + splits + 1, 0)),
            ]
            + [piece] * 4,
            out_specs=(piece, pl.BlockSpec((8, 128), lambda i, ids, pair, high: (0, 0))),
        ),
        name=f"finish{b}",
    )(ids, pair, high, codes, codes, *parts)


def subtract_kernel(peak_ref, *refs):
    out_ref = refs[-1]
    for b, ref in enumerate(refs[:-1]):
        out_ref[b] = ref[...] - peak_ref[b : b + 1, 0:1]


def subtract(peak, insides):
    return pl.pallas_call(
        subtract_kernel,
        out_shape=jax.ShapeDtypeStruct((len(insides),) + insides[0].shape, F32),
        name="subtract",
    )(peak, *insides)


def largest(value):
    def among(v, axis, count, shifts):
        return functools.reduce(jnp.maximum, [lax.ppermute(v, axis, shift(count, d)) for d in shifts], v)

    value = among(value, "core", 2, (1,))
    value = among(value, "x", 4, (1, 2, 3))
    value = among(value, "y", 4, (1, 2, 3))
    value = among(value, "z", 8, (1, 2, 3))
    return among(value, "z", 8, (4,))


def local(left_mant, right_mant, left_scale, right_scale, rule_probs, pair_logp, nucleotides, first_block):
    count, splits, nt, rows = left_mant.shape[:4]
    depth, cols = left_mant.shape[5], right_mant.shape[5]
    nz = lax.axis_size("z")
    core = lax.axis_index("core")
    ids = jnp.stack([lax.axis_index("z"), core, lax.axis_index("y"), lax.axis_index("x"), first_block[0]]).astype(
        jnp.int32
    )

    own = right_mant.reshape(count, splits, nt, right_mant.shape[4], cols)
    sibling = lax.ppermute(own, "core", SWAP)
    chip = jnp.concatenate(
        [jnp.where(core == 0, own, sibling), jnp.where(core == 0, sibling, own)], axis=3
    )
    blocks = [chip[b] for b in range(count)]

    keep, send = pick(ids, left_mant.reshape(count, splits * nt * rows, depth), nz)
    got = lax.ppermute(send, "core", SWAP)

    near = list(blocks)
    pieces = [[] for _ in range(count)]
    for step in range(3):
        for b in range(count):
            near[b] = lax.ppermute(near[b], ZC, ring_pairs(nz))
            pieces[b].append(near[b])
    far = [lax.ppermute(near[b], ZC, ring_pairs(nz, (1 - OWNER[b],))) for b in range(count)]

    up = [lax.ppermute(v, "y", shift(4, 1)) for v in (keep, got)]
    down = [lax.ppermute(v, "y", shift(4, -1)) for v in (keep, got)]
    across = [lax.ppermute(up[0], "y", shift(4, 1)), lax.ppermute(down[1], "y", shift(4, -1))]
    mine = (keep, down[0], across[0], up[0])
    theirs = (got, down[1], across[1], up[1])

    total_scale = left_scale + right_scale
    highest = jnp.max(total_scale, axis=1)
    weight = jnp.exp(total_scale - highest[:, None])
    mixing = (rule_probs[None, None] * weight[:, :, None, None, None]).astype(BF16)
    table = jnp.swapaxes(mixing, 3, 4).reshape(count, splits, nt * nt, nt)
    lane = jnp.arange(nt * rows)
    spread = (lane[None, :] // rows == jnp.arange(nt)[:, None]).astype(BF16)
    wide = jnp.einsum("bsry,yl->bsrl", table, spread, preferred_element_type=F32)
    same = lane[None, :] % rows == jnp.arange(rows)[:, None]
    kron = jnp.where(same, wide[:, :, :, None, :], 0.0).astype(BF16)
    kron = kron.reshape(count, splits, nt * nt * rows, nt * rows)

    pair = pair_logp.reshape(-1)
    codes = nucleotides.reshape(-1, 128)
    insides, peaks = [], []
    for b in range(count):
        mixed = mix(b, kron, mine, theirs, nt)
        kept, sent = contract(b, ids, mixed, pieces[b], blocks[b], far[b], nt)
        arrived = lax.ppermute(sent, "core", SWAP)
        parts = add_cores(b, ids, kept, arrived)
        parts = [parts[0]] + [lax.ppermute(parts[d], "x", shift(4, d)) for d in (1, 2, 3)]
        inside, peak = finish(b, ids, pair, highest, codes, parts, splits)
        insides.append(inside)
        peaks.append(peak[:1])
    peak = largest(jnp.concatenate(peaks, axis=0))
    return subtract(peak, insides), peak[:, 0]


def solution(mesh):
    split = Mesh(
        mesh.devices.reshape(8, 2, mesh.shape["col"], mesh.shape["layer"]),
        ("z", "core", "y", "x"),
    )
    in_specs = (
        P(None, None, None, ("z", "core", "y"), "x", None),
        P(None, None, None, "x", ("z", "core"), "y"),
        P(),
        P(),
        P(),
        P(),
        P(),
        P(),
    )
    out_specs = (P(None, None, ("z", "core", "x"), "y"), P())
    return jax.shard_map(local, mesh=split, in_specs=in_specs, out_specs=out_specs, check_vma=False)
```

```python
import functools

import jax
import jax.numpy as jnp
from jax import lax
from jax.experimental import pallas as pl
from jax.experimental.pallas import tpu as pltpu
from jax.sharding import Mesh
from jax.sharding import PartitionSpec as P


ZC = ("z", "core")
CHUNKS = ((0, 0, 5, 0), (1, 0, 5, 1), (2, 0, 4, 0), (2, 4, 5, 1))
F32 = jnp.float32
BF16 = jnp.bfloat16


def shift(count, by):
    return [(i, (i + by) % count) for i in range(count)]


SWAP = [(0, 1), (1, 0)]


def ring_pairs(nz, cores=(0, 1)):
    pairs = []
    for z in range(nz):
        if 0 in cores:
            pairs.append((2 * z, 2 * ((z + 1) % nz)))
        if 1 in cores:
            pairs.append((2 * z + 1, 2 * ((z - 1) % nz) + 1))
    return pairs


def wanted_positions(z, who, owner, column, nz, width):
    piece, within = column // width, column % width
    step = jnp.where(who == 0, -1, 1) * (piece + 1)
    last = jnp.where(who == owner, 0, nz // 2)
    block = (z + jnp.where(piece == 3, last, step) + 2 * nz) % nz
    return block * width + within


def pick_kernel(nz, unit, ids_ref, left_ref, keep_ref, send_ref):
    z, core = ids_ref[0], ids_ref[1]
    depth = left_ref.shape[2]
    half = depth // 2
    row = lax.broadcasted_iota(jnp.int32, (depth, half), 0)
    column = lax.broadcasted_iota(jnp.int32, (1, half), 1)
    chosen = {}
    for b, first, end, owner in CHUNKS:
        span = slice(first * unit, end * unit)
        for who, out in ((core, keep_ref), (1 - core, send_ref)):
            key = (owner, out is keep_ref)
            if key not in chosen:
                source = wanted_positions(z, who, owner, column, nz, half // 4)
                chosen[key] = jnp.where(row == source, 1.0, 0.0).astype(BF16)
            out[b, span] = jnp.dot(left_ref[b, span], chosen[key], preferred_element_type=F32).astype(BF16)


def pick(ids, left, nz, unit):
    b, rows, depth = left.shape
    out = jax.ShapeDtypeStruct((b, rows, depth // 2), BF16)
    return pl.pallas_call(
        functools.partial(pick_kernel, nz, unit),
        out_shape=(out, out),
        in_specs=[pl.BlockSpec(memory_space=pltpu.SMEM), pl.BlockSpec(memory_space=pltpu.VMEM)],
        out_specs=(pl.BlockSpec(memory_space=pltpu.VMEM),) * 2,
        name="pick",
    )(ids, left)


def contract_kernel(nt, owner, carry, last, ids_ref, kron_ref, *refs):
    mine, theirs, (p1, p2, p3, own, far) = refs[:4], refs[4:8], refs[8:13]
    refs = refs[13:]
    before, refs = (refs[0], refs[1:]) if carry else (None, refs)
    outs, mixed, acc = refs[:-2], refs[-2], refs[-1]
    s = pl.program_id(0)
    kron = kron_ref[0, 0]
    for d in range(4):
        rhs = jnp.concatenate([mine[d][0], theirs[d][0]], axis=1)
        o = jnp.dot(kron, rhs, preferred_element_type=F32).astype(BF16)
        for x in range(nt):
            for z in range(nt):
                top = (x * nt + z) * 16
                for r in range(2):
                    at = x * 128 + r * 64 + d * 16
                    mixed[at : at + 16, z * 128 : (z + 1) * 128] = o[top : top + 16, r * 128 : (r + 1) * 128]
    end = jnp.where(ids_ref[1] == owner, own[0], far[0])
    rhs = jnp.concatenate([p1[0], p2[0], p3[0], end], axis=1)
    rhs = rhs.reshape(rhs.shape[0] * rhs.shape[1], rhs.shape[2])
    part = jnp.dot(mixed[...], rhs, preferred_element_type=F32)

    @pl.when(s == 0)
    def _():
        acc[...] = part + before[...] if carry else part

    @pl.when(s > 0)
    def _():
        acc[...] += part

    @pl.when(s == pl.num_programs(0) - 1)
    def _():
        if last:
            y, x = ids_ref[2], ids_ref[3]
            for i, out in enumerate(outs):
                at = (x + i % 4 - y + 4) % 4 * 16 + i // 4 * 64
                for n in range(nt):
                    out[n] = acc[pl.ds(pl.multiple_of(n * 128 + at, 16), 16), :]
        else:
            outs[0][...] = acc[...]


def contract(chunk, ids, kron, mine, theirs, pieces, own, far, nt, before, last):
    b, first, end, owner = chunk
    cols = own.shape[3]
    wide = nt * 128
    rows = nt * 16
    left = pl.BlockSpec((1, rows, 128), lambda s, ids: (b, s + first, 0))
    piece = pl.BlockSpec((1,) + own.shape[1:], lambda s, ids: (s, 0, 0, 0))
    total = pl.BlockSpec((wide, cols), lambda s, ids: (0, 0))
    part = pl.BlockSpec((nt, 16, cols), lambda s, ids: (0, 0, 0))
    carry = before is not None
    return pl.pallas_call(
        functools.partial(contract_kernel, nt, owner, carry, last),
        out_shape=(jax.ShapeDtypeStruct((nt, 16, cols), F32),) * 8 if last else jax.ShapeDtypeStruct((wide, cols), F32),
        grid_spec=pltpu.PrefetchScalarGridSpec(
            num_scalar_prefetch=1,
            grid=(end - first,),
            in_specs=[pl.BlockSpec((1, 1, nt * rows, rows), lambda s, ids: (b, s + first, 0, 0))]
            + [left] * 8
            + [piece] * 5
            + [total] * carry,
            out_specs=(part,) * 8 if last else total,
            scratch_shapes=[pltpu.VMEM((wide, wide), BF16), pltpu.VMEM((wide, cols), F32)],
        ),
        name=f"contract{b}{first}",
    )(ids, kron, *mine, *theirs, *pieces, own, far, *((before,) if carry else ()))


def finish_kernel(b, ids_ref, pair_ref, high_ref, row_ref, col_ref, *refs):
    parts, peaks, out_ref, max_ref = refs[:8], refs[8], refs[9], refs[10]
    z, core, y, x = ids_ref[0], ids_ref[1], ids_ref[2], ids_ref[3]
    nt, rows, cols = out_ref.shape
    start = ((z * 2 + core) * 4 + x) * rows
    line = row_ref[pl.ds(start // 128, 1), :].astype(F32)
    lane = lax.broadcasted_iota(jnp.int32, (rows, 128), 1)
    sub = lax.broadcasted_iota(jnp.int32, (rows, 128), 0)
    code = jnp.sum(jnp.where(lane == start % 128 + sub, line, 0.0), axis=1, keepdims=True)
    first = y * (cols // 128)
    column = jnp.concatenate([col_ref[pl.ds(first + n, 1), :] for n in range(cols // 128)], axis=1)
    high = high_ref[b]
    best = None
    for n in range(nt):
        def factor(u):
            base = (n * 4 + u) * 4
            t = jnp.where(column == 0, pair_ref[base], pair_ref[base + 1])
            t = jnp.where(column == 2, pair_ref[base + 2], t)
            return jnp.where(column == 3, pair_ref[base + 3], t)

        pairing = jnp.where(code == 0.0, factor(0), factor(1))
        pairing = jnp.where(code == 2.0, factor(2), pairing)
        pairing = jnp.where(code == 3.0, factor(3), pairing)
        summed = functools.reduce(lambda a, c: a + c, [part[n] for part in parts])
        inside = high + jnp.log(summed) + pairing
        out_ref[n] = inside
        best = inside if best is None else jnp.maximum(best, inside)
    best = jnp.max(best, axis=1, keepdims=True)
    best = jnp.max(best, axis=0, keepdims=True)
    row = lax.broadcasted_iota(jnp.int32, max_ref.shape, 0)
    max_ref[...] = jnp.where(row == b, best, peaks[...])


def finish(b, ids, pair, high, codes, parts, peaks, splits):
    nt, rows, cols = parts[0].shape
    piece = pl.BlockSpec((nt, rows, cols), lambda i, ids, pair, high: (0, 0, 0))
    return pl.pallas_call(
        functools.partial(finish_kernel, b),
        out_shape=(jax.ShapeDtypeStruct((nt, rows, cols), F32), jax.ShapeDtypeStruct((8, 128), F32)),
        grid_spec=pltpu.PrefetchScalarGridSpec(
            num_scalar_prefetch=3,
            grid=(1,),
            in_specs=[
                pl.BlockSpec((8, 128), lambda i, ids, pair, high: (ids[4] + b, 0)),
                pl.BlockSpec((8, 128), lambda i, ids, pair, high: (ids[4] + b + splits + 1, 0)),
            ]
            + [piece] * 8
            + [pl.BlockSpec((8, 128), lambda i, ids, pair, high: (0, 0))],
            out_specs=(piece, pl.BlockSpec((8, 128), lambda i, ids, pair, high: (0, 0))),
        ),
        name=f"finish{b}",
    )(ids, pair, high, codes, codes, *parts, peaks)


def subtract_kernel(peak_ref, *refs):
    insides, out_ref, scale_ref = refs[:-2], refs[-2], refs[-1]
    for b, ref in enumerate(insides):
        out_ref[b] = ref[...] - peak_ref[b, 0]
        scale_ref[b] = peak_ref[b, 0]


def subtract(peak, insides):
    return pl.pallas_call(
        subtract_kernel,
        out_shape=(
            jax.ShapeDtypeStruct((len(insides),) + insides[0].shape, F32),
            jax.ShapeDtypeStruct((len(insides),), F32),
        ),
        in_specs=[pl.BlockSpec(memory_space=pltpu.SMEM)] + [pl.BlockSpec(memory_space=pltpu.VMEM)] * len(insides),
        out_specs=(pl.BlockSpec(memory_space=pltpu.VMEM), pl.BlockSpec(memory_space=pltpu.SMEM)),
        name="subtract",
    )(peak, *insides)


def largest(value):
    def among(v, axis, count, shifts):
        return functools.reduce(jnp.maximum, [lax.ppermute(v, axis, shift(count, d)) for d in shifts], v)

    value = among(value, "core", 2, (1,))
    value = among(value, "x", 4, (1, 2, 3))
    value = among(value, "y", 4, (1, 2, 3))
    value = among(value, "z", 8, (1, 7))
    return among(value, "z", 8, (3, 5))


def local(left_mant, right_mant, left_scale, right_scale, rule_probs, pair_logp, nucleotides, first_block):
    count, splits, nt, rows = left_mant.shape[:4]
    depth, cols = left_mant.shape[5], right_mant.shape[5]
    nz = lax.axis_size("z")
    core = lax.axis_index("core")
    ids = jnp.stack([lax.axis_index("z"), core, lax.axis_index("y"), lax.axis_index("x"), first_block[0]]).astype(
        jnp.int32
    )

    own = right_mant.reshape(count, splits, nt, right_mant.shape[4], cols)
    sibling = lax.ppermute(own, "core", SWAP)
    chip = jnp.concatenate(
        [jnp.where(core == 0, own, sibling), jnp.where(core == 0, sibling, own)], axis=3
    )
    blocks = [chip[b, first:end] for b, first, end, _ in CHUNKS]

    keep, send = pick(ids, left_mant.reshape(count, splits * nt * rows, depth), nz, nt * rows)
    got = lax.ppermute(send, "core", SWAP)

    near = list(blocks)
    pieces = [[] for _ in CHUNKS]
    for step in range(3):
        for c in range(len(CHUNKS)):
            near[c] = lax.ppermute(near[c], ZC, ring_pairs(nz))
            pieces[c].append(near[c])
        if step == 0:
            *near, keep, send = lax.optimization_barrier((*near, keep, send))
            for c in range(len(CHUNKS)):
                pieces[c] = [near[c]]
    far = [lax.ppermute(near[c], ZC, ring_pairs(nz, (1 - chunk[3],))) for c, chunk in enumerate(CHUNKS)]

    up = [lax.ppermute(v, "y", shift(4, 1)) for v in (keep, got)]
    down = [lax.ppermute(v, "y", shift(4, -1)) for v in (keep, got)]
    across = [lax.ppermute(up[0], "y", shift(4, 1)), lax.ppermute(down[1], "y", shift(4, -1))]
    mine = (keep, down[0], across[0], up[0])
    theirs = (got, down[1], across[1], up[1])

    total_scale = left_scale + right_scale
    highest = jnp.max(total_scale, axis=1)
    weight = jnp.exp(total_scale - highest[:, None])
    mixing = (rule_probs[None, None] * weight[:, :, None, None, None]).astype(BF16)
    table = jnp.swapaxes(mixing, 3, 4).reshape(count, splits, nt * nt, nt)
    lane = jnp.arange(nt * rows)
    spread = (lane[None, :] // rows == jnp.arange(nt)[:, None]).astype(BF16)
    wide = jnp.einsum("bsry,yl->bsrl", table, spread, preferred_element_type=F32)
    same = lane[None, :] % rows == jnp.arange(rows)[:, None]
    kron = jnp.where(same, wide[:, :, :, None, :], 0.0).astype(BF16)
    kron = kron.reshape(count, splits, nt * nt * rows, nt * rows)

    pair = pair_logp.reshape(-1)
    codes = nucleotides.reshape(-1, 128)
    insides, peak, parts = [], jnp.zeros((8, 128), F32), None
    for c, chunk in enumerate(CHUNKS):
        b, last = chunk[0], chunk[2] == splits
        parts = contract(chunk, ids, kron, mine, theirs, pieces[c], blocks[c], far[c], nt, parts, last)
        if last:
            sums = [parts[0]]
            for i in range(1, 8):
                pairs = [(q * 4 + x, (q ^ (i // 4)) * 4 + (x + i % 4) % 4) for q in range(2) for x in range(4)]
                sums.append(lax.ppermute(parts[i], ("core", "x"), pairs))
            inside, peak = finish(b, ids, pair, highest, codes, sums, peak, splits)
            insides.append(inside)
            parts = None
    return subtract(largest(peak), insides)


def solution(mesh):
    split = Mesh(
        mesh.devices.reshape(8, 2, mesh.shape["col"], mesh.shape["layer"]),
        ("z", "core", "y", "x"),
    )
    in_specs = (
        P(None, None, None, ("z", "core", "y"), "x", None),
        P(None, None, None, "x", ("z", "core"), "y"),
        P(),
        P(),
        P(),
        P(),
        P(),
        P(),
    )
    out_specs = (P(None, None, ("z", "core", "x"), "y"), P())
    return jax.shard_map(local, mesh=split, in_specs=in_specs, out_specs=out_specs, check_vma=False)
```

```python
import functools

import jax
import jax.numpy as jnp
from jax import lax
from jax.experimental import pallas as pl
from jax.experimental.pallas import tpu as pltpu
from jax.sharding import Mesh
from jax.sharding import PartitionSpec as P


ZC = ("z", "core")
CHUNKS = ((0, 0, 5, 0), (1, 0, 5, 0), (2, 0, 5, 1))
GROUPS = ((0,), (1,), (2,))
F32 = jnp.float32
BF16 = jnp.bfloat16


def shift(count, by):
    return [(i, (i + by) % count) for i in range(count)]


SWAP = [(0, 1), (1, 0)]


def room(mib):
    return pltpu.CompilerParams(vmem_limit_bytes=mib * 2**20)


def small(count):
    return [pl.BlockSpec(memory_space=pltpu.SMEM)] * count


def near(count):
    return [pl.BlockSpec(memory_space=pltpu.VMEM)] * count


def ring_pairs(nz, cores=(0, 1)):
    pairs = []
    for z in range(nz):
        if 0 in cores:
            pairs.append((2 * z, 2 * ((z + 1) % nz)))
        if 1 in cores:
            pairs.append((2 * z + 1, 2 * ((z - 1) % nz) + 1))
    return pairs


def wanted_positions(z, who, owner, column, nz, width):
    piece, within = column // width, column % width
    step = jnp.where(who == 0, -1, 1) * (piece + 1)
    last = jnp.where(who == owner, 0, nz // 2)
    block = (z + jnp.where(piece == 3, last, step) + 2 * nz) % nz
    return block * width + within


def cross_pairs(nz):
    return [(2 * z + q, 2 * ((z + (1 if q else -1)) % nz) + 1 - q) for z in range(nz) for q in range(2)]


def pick_kernel(nz, unit, ids_ref, left_ref, keep_ref, send_ref):
    z, core = ids_ref[0], ids_ref[1]
    depth = left_ref.shape[2]
    half = depth // 2
    row = lax.broadcasted_iota(jnp.int32, (depth, half), 0)
    column = lax.broadcasted_iota(jnp.int32, (1, half), 1)
    chosen = {}
    for b, first, end, owner in CHUNKS:
        span = slice(first * unit, end * unit)
        for who, out in ((core, keep_ref), (1 - core, send_ref)):
            key = (owner, out is keep_ref)
            if key not in chosen:
                source = wanted_positions(z, who, owner, column, nz, half // 4)
                chosen[key] = jnp.where(row == source, 1.0, 0.0).astype(BF16)
            out[b, span] = jnp.dot(left_ref[b, span], chosen[key], preferred_element_type=F32).astype(BF16)


def pick(ids, left, nz, unit):
    b, rows, depth = left.shape
    out = jax.ShapeDtypeStruct((b, rows, depth // 2), BF16)
    return pl.pallas_call(
        functools.partial(pick_kernel, nz, unit),
        out_shape=(out, out),
        in_specs=[pl.BlockSpec(memory_space=pltpu.SMEM), pl.BlockSpec(memory_space=pltpu.VMEM)],
        out_specs=(pl.BlockSpec(memory_space=pltpu.VMEM),) * 2,
        compiler_params=room(8),
        name="pick",
    )(ids, left)


def mix_kernel(nt, b, weight_ref, rules_ref, *refs):
    mine, theirs, mixed = refs[:4], refs[4:8], refs[8]
    splits, (pairs, lanes) = mixed.shape[0], rules_ref.shape
    same = lax.broadcasted_iota(jnp.int32, (16, lanes), 1) % 16 == lax.broadcasted_iota(jnp.int32, (16, lanes), 0)

    def one_split(s, _):
        mixing = rules_ref[...] * weight_ref[b, s]
        kron = jnp.where(same[None], mixing[:, None, :], 0.0).reshape(pairs * 16, lanes).astype(BF16)
        at = pl.ds(pl.multiple_of(s * lanes, 16), lanes)
        for d in range(4):
            rhs = jnp.concatenate([mine[d][b, at, :], theirs[d][b, at, :]], axis=1)
            o = jnp.dot(kron, rhs, preferred_element_type=F32).astype(BF16)
            for x in range(nt):
                for z in range(nt):
                    top = (x * nt + z) * 16
                    for r in range(2):
                        row = x * 128 + r * 64 + d * 16
                        mixed[s, row : row + 16, z * 128 : (z + 1) * 128] = o[top : top + 16, r * 128 : (r + 1) * 128]
        return 0

    lax.fori_loop(0, splits, one_split, 0)


def mix(b, weight, rules, mine, theirs, nt):
    return pl.pallas_call(
        functools.partial(mix_kernel, nt, b),
        out_shape=jax.ShapeDtypeStruct((weight.shape[1], nt * 128, nt * 128), BF16),
        in_specs=small(1) + near(9),
        out_specs=near(1)[0],
        compiler_params=room(16),
    )(weight, rules, *mine, *theirs)


def contract_kernel(nt, owner, ids_ref, mixed, p1, p2, p3, own, far, keep_ref, send_ref, acc):
    mine = ids_ref[1] == owner

    def product(s):
        rhs = jnp.concatenate([p1[s], p2[s], p3[s], jnp.where(mine, own[s], far[s])], axis=1)
        rhs = rhs.reshape(nt * 128, rhs.shape[2])
        return jnp.dot(mixed[s], rhs, preferred_element_type=F32).reshape(acc.shape)

    acc[...] = product(0)

    def more(s, _):
        acc[...] += product(s)
        return 0

    last = mixed.shape[0] - 1
    lax.fori_loop(1, last, more, 0)
    total = acc[...] + product(last)
    keep_ref[0] = total[:, :64]
    send_ref[0] = total[:, 64:]


def contract(b, ids, mixed, pieces, own, far, nt):
    cols = own.shape[3]
    out = jax.ShapeDtypeStruct((1, nt, 64, cols), F32)
    return pl.pallas_call(
        functools.partial(contract_kernel, nt, CHUNKS[b][3]),
        out_shape=(out, out),
        in_specs=small(1) + near(6),
        out_specs=tuple(near(2)),
        scratch_shapes=[pltpu.VMEM((nt, 128, cols), F32)],
        compiler_params=room(16),
    )(ids, mixed, *pieces, own, far)


def add_kernel(ids_ref, keep_ref, got_ref, *outs):
    y, x = ids_ref[2], ids_ref[3]
    for d, out in enumerate(outs):
        at = (x + d - y + 4) % 4
        rows = pl.ds(pl.multiple_of(at * 16, 16), 16)
        out[...] = keep_ref[:, :, rows, :] + got_ref[:, :, rows, :]


def add_cores(ids, keep, got):
    size, nt, rows, cols = keep.shape
    return pl.pallas_call(
        add_kernel,
        out_shape=(jax.ShapeDtypeStruct((size, nt, rows // 4, cols), F32),) * 4,
        in_specs=[pl.BlockSpec(memory_space=pltpu.SMEM)] + [pl.BlockSpec(memory_space=pltpu.VMEM)] * 2,
        out_specs=(pl.BlockSpec(memory_space=pltpu.VMEM),) * 4,
        compiler_params=room(6),
    )(ids, keep, got)


def pairs_kernel(nt, splits, ids_ref, pair_ref, rule_ref, high_ref, codes_ref, *outs):
    outs, rules_ref = outs[:-1], outs[-1]
    group = lax.broadcasted_iota(jnp.int32, (1, rules_ref.shape[1]), 1) // 16
    for n in range(nt):
        for m in range(nt):
            line = jnp.full(group.shape, rule_ref[n, 0, m], F32)
            for y in range(1, nt):
                line = jnp.where(group == y, rule_ref[n, y, m], line)
            rules_ref[n * nt + m : n * nt + m + 1, :] = line
    z, core, y, x = ids_ref[0], ids_ref[1], ids_ref[2], ids_ref[3]
    _, _, rows, cols = outs[0].shape
    start = ((z * 2 + core) * 4 + x) * rows
    lane = lax.broadcasted_iota(jnp.int32, (rows, 128), 1)
    sub = lax.broadcasted_iota(jnp.int32, (rows, 128), 0)
    first = y * (cols // 128)
    for b, (out, at) in enumerate((out, at) for out in outs for at in range(out.shape[0])):
        row_block = (ids_ref[4] + b) * 8
        col_block = (ids_ref[4] + b + splits + 1) * 8
        line = codes_ref[pl.ds(row_block + start // 128, 1), :].astype(F32)
        code = jnp.sum(jnp.where(lane == start % 128 + sub, line, 0.0), axis=1, keepdims=True)
        column = jnp.concatenate(
            [codes_ref[pl.ds(col_block + first + n, 1), :] for n in range(cols // 128)], axis=1
        )
        high = high_ref[b]
        for n in range(nt):

            def factor(u):
                t = jnp.where(column == 0, pair_ref[u, 0, n], pair_ref[u, 1, n])
                t = jnp.where(column == 2, pair_ref[u, 2, n], t)
                return jnp.where(column == 3, pair_ref[u, 3, n], t)

            pairing = jnp.where(code == 0.0, factor(0), factor(1))
            pairing = jnp.where(code == 2.0, factor(2), pairing)
            out[at, n] = jnp.where(code == 3.0, factor(3), pairing) + high


def pairs_of(ids, pair, rule, high, codes, splits, nt, rows, cols):
    return pl.pallas_call(
        functools.partial(pairs_kernel, nt, splits),
        out_shape=tuple(jax.ShapeDtypeStruct((len(group), nt, rows, cols), F32) for group in GROUPS)
        + (jax.ShapeDtypeStruct((nt * nt, nt * rows), F32),),
        in_specs=small(4) + near(1),
        out_specs=tuple(near(len(GROUPS) + 1)),
        compiler_params=room(6),
        name="pairs",
    )(ids, pair, rule, high, codes)


def finish_kernel(group, pairing_ref, *refs):
    parts, peaks_ref, out_ref, max_ref = refs[:4], refs[4:-2], refs[-2], refs[-1]
    lane = lax.broadcasted_iota(jnp.int32, (1, 128), 1)
    row = peaks_ref[0][...] if peaks_ref else jnp.full((1, 128), -jnp.inf, F32)
    for at, b in enumerate(group):
        best = None
        for n in range(out_ref.shape[1]):
            total = (parts[0][at, n] + parts[1][at, n]) + (parts[2][at, n] + parts[3][at, n])
            inside = jnp.log(total) + pairing_ref[at, n]
            out_ref[at, n] = inside
            best = inside if best is None else jnp.maximum(best, inside)
        best = jnp.max(best, axis=1, keepdims=True)
        best = jnp.max(best, axis=0, keepdims=True)
        row = jnp.where(lane == b, best, row)
    max_ref[...] = row


def finish(group, pairing, parts, peaks):
    return pl.pallas_call(
        functools.partial(finish_kernel, group),
        out_shape=(jax.ShapeDtypeStruct(pairing.shape, F32), jax.ShapeDtypeStruct((1, 128), F32)),
        in_specs=[pl.BlockSpec(memory_space=pltpu.VMEM)] * (5 + len(peaks)),
        out_specs=(pl.BlockSpec(memory_space=pltpu.VMEM),) * 2,
        compiler_params=room(6),
    )(pairing, *parts, *peaks)


def subtract_kernel(tops_ref, *refs):
    insides, out_ref, scale_ref = refs[:-2], refs[-2], refs[-1]
    top = jnp.max(tops_ref[...], axis=0)
    lane = lax.broadcasted_iota(jnp.int32, top.shape, 1)
    for b, (ref, at) in enumerate((ref, at) for ref in insides for at in range(ref.shape[0])):
        out_ref[b] = ref[at] - top[:, b : b + 1]
        scale_ref[b] = jnp.max(jnp.where(lane == b, top, -jnp.inf))


def subtract(tops, insides):
    return pl.pallas_call(
        subtract_kernel,
        out_shape=(
            jax.ShapeDtypeStruct((len(CHUNKS),) + insides[0].shape[1:], F32),
            jax.ShapeDtypeStruct((len(CHUNKS),), F32),
        ),
        in_specs=[pl.BlockSpec(memory_space=pltpu.VMEM)] * (1 + len(insides)),
        out_specs=(pl.BlockSpec(memory_space=pltpu.VMEM), pl.BlockSpec(memory_space=pltpu.SMEM)),
        compiler_params=room(6),
        name="subtract",
    )(tops, *insides)


def compute(left_mant, right_mant, left_scale, right_scale, rule_probs, pair_logp, nucleotides, first_block):
    count, splits, nt, rows = left_mant.shape[:4]
    depth, cols = left_mant.shape[5], right_mant.shape[5]
    nz = lax.axis_size("z")
    core = lax.axis_index("core")
    ids = jnp.stack([lax.axis_index("z"), core, lax.axis_index("y"), lax.axis_index("x"), first_block[0]]).astype(
        jnp.int32
    )

    own = right_mant.reshape(count, splits, nt, right_mant.shape[4], cols)
    sibling = lax.ppermute(own, "core", SWAP)

    def by_core(same, other):
        return jnp.concatenate([jnp.where(core == 0, same, other), jnp.where(core == 0, other, same)], axis=-2)

    chip = by_core(own, sibling)
    blocks = [chip[b] for b in range(count)]
    pieces, far = [], []
    for c, chunk in enumerate(CHUNKS):
        line = [blocks[c]]
        if c == 0:
            same = lax.ppermute(own[0], ZC, ring_pairs(nz))
            line.append(by_core(same, lax.ppermute(own[0], ZC, cross_pairs(nz))))
        for _ in range(len(line), 4):
            line.append(lax.ppermute(line[-1], ZC, ring_pairs(nz)))
        pieces.append(line[1:])
        far.append(lax.ppermute(line[-1], ZC, ring_pairs(nz, (1 - chunk[3],))))

    keep, give = pick(ids, left_mant.reshape(count, splits * nt * rows, depth), nz, nt * rows)
    got = lax.ppermute(give, "core", SWAP)
    up = [lax.ppermute(v, "y", shift(4, 1)) for v in (keep, got)]
    down = [lax.ppermute(v, "y", shift(4, -1)) for v in (keep, got)]
    across = [lax.ppermute(up[0], "y", shift(4, 1)), lax.ppermute(down[1], "y", shift(4, -1))]
    mine = (keep, down[0], across[0], up[0])
    theirs = (got, down[1], across[1], up[1])

    total_scale = left_scale + right_scale
    highest = jnp.max(total_scale, axis=1)
    weight = jnp.exp(total_scale - highest[:, None])
    *pairings, rules = pairs_of(
        ids,
        jnp.transpose(pair_logp, (1, 2, 0)),
        rule_probs,
        highest,
        nucleotides.reshape(-1, 128),
        splits,
        nt,
        rows,
        cols,
    )
    insides, peaks = [], ()
    for g, group in enumerate(GROUPS):
        kept, sent = contract(g, ids, mix(g, weight, rules, mine, theirs, nt), pieces[g], blocks[g], far[g], nt)
        parts = add_cores(ids, kept, lax.ppermute(sent, "core", SWAP))
        sums = [parts[0]] + [lax.ppermute(parts[d], "x", shift(4, d)) for d in (1, 2, 3)]
        inside, peak = finish(group, pairings[g], sums, peaks)
        peaks = (peak,)
        insides.append(inside)
    everyone = ("z", "core", "y", "x")
    tops = jnp.broadcast_to(peaks[0][None], (lax.axis_size(everyone), 1, 128))
    tops = lax.all_to_all(tops, everyone, split_axis=0, concat_axis=0, tiled=True)
    return subtract(tops, insides)


def solution(mesh):
    split = Mesh(
        mesh.devices.reshape(8, 2, mesh.shape["col"], mesh.shape["layer"]),
        ("z", "core", "y", "x"),
    )
    in_specs = (
        P(None, None, None, ("z", "core", "y"), "x", None),
        P(None, None, None, "x", ("z", "core"), "y"),
        P(),
        P(),
        P(),
        P(),
        P(),
        P(),
    )
    out_specs = (P(None, None, ("z", "core", "x"), "y"), P())
    return jax.shard_map(compute, mesh=split, in_specs=in_specs, out_specs=out_specs, check_vma=False)
```

```python
import functools

import jax
import jax.numpy as jnp
from jax import lax
from jax.experimental import pallas as pl
from jax.experimental.pallas import tpu as pltpu
from jax.sharding import Mesh
from jax.sharding import PartitionSpec as P


ZC = ("z", "core")
OWNERS = (((0, 5, 0),), ((0, 5, 1),), ((0, 3, 0), (3, 5, 1)))
GROUPS = ((0,), (1,), (2,))
F32 = jnp.float32
BF16 = jnp.bfloat16


def shift(count, by):
    return [(i, (i + by) % count) for i in range(count)]


SWAP = [(0, 1), (1, 0)]


def room(mib):
    return pltpu.CompilerParams(vmem_limit_bytes=mib * 2**20)


def small(count):
    return [pl.BlockSpec(memory_space=pltpu.SMEM)] * count


def near(count):
    return [pl.BlockSpec(memory_space=pltpu.VMEM)] * count


def ring_pairs(nz, cores=(0, 1)):
    pairs = []
    for z in range(nz):
        if 0 in cores:
            pairs.append((2 * z, 2 * ((z + 1) % nz)))
        if 1 in cores:
            pairs.append((2 * z + 1, 2 * ((z - 1) % nz) + 1))
    return pairs


def wanted_positions(z, who, owner, column, nz, width):
    piece, within = column // width, column % width
    step = jnp.where(who == 0, -1, 1) * (piece + 1)
    last = jnp.where(who == owner, 0, nz // 2)
    block = (z + jnp.where(piece == 3, last, step) + 2 * nz) % nz
    return block * width + within


def cross_pairs(nz):
    return [(2 * z + q, 2 * ((z + (1 if q else -1)) % nz) + 1 - q) for z in range(nz) for q in range(2)]


def pick_kernel(nz, unit, ids_ref, left_ref, keep_ref, send_ref):
    z, core = ids_ref[0], ids_ref[1]
    depth = left_ref.shape[2]
    half = depth // 2
    row = lax.broadcasted_iota(jnp.int32, (depth, half), 0)
    column = lax.broadcasted_iota(jnp.int32, (1, half), 1)
    chosen = {}
    for b, (first, end, owner) in ((b, part) for b, parts in enumerate(OWNERS) for part in parts):
        span = slice(first * unit, end * unit)
        for who, out in ((core, keep_ref), (1 - core, send_ref)):
            key = (owner, out is keep_ref)
            if key not in chosen:
                source = wanted_positions(z, who, owner, column, nz, half // 4)
                chosen[key] = jnp.where(row == source, 1.0, 0.0).astype(BF16)
            out[b, span] = jnp.dot(left_ref[b, span], chosen[key], preferred_element_type=F32).astype(BF16)


def pick(ids, left, nz, unit):
    b, rows, depth = left.shape
    out = jax.ShapeDtypeStruct((b, rows, depth // 2), BF16)
    return pl.pallas_call(
        functools.partial(pick_kernel, nz, unit),
        out_shape=(out, out),
        in_specs=[pl.BlockSpec(memory_space=pltpu.SMEM), pl.BlockSpec(memory_space=pltpu.VMEM)],
        out_specs=(pl.BlockSpec(memory_space=pltpu.VMEM),) * 2,
        compiler_params=room(3),
        name="pick",
    )(ids, left)


def mix_kernel(nt, b, weight_ref, rules_ref, *refs):
    mine, theirs, mixed = refs[:4], refs[4:8], refs[8]
    splits, (pairs, lanes) = mixed.shape[0], rules_ref.shape
    same = lax.broadcasted_iota(jnp.int32, (16, lanes), 1) % 16 == lax.broadcasted_iota(jnp.int32, (16, lanes), 0)

    def one_split(s, _):
        mixing = rules_ref[...] * weight_ref[b, s]
        kron = jnp.where(same[None], mixing[:, None, :], 0.0).reshape(pairs * 16, lanes).astype(BF16)
        at = pl.ds(pl.multiple_of(s * lanes, 16), lanes)
        for d in range(4):
            rhs = jnp.concatenate([mine[d][b, at, :], theirs[d][b, at, :]], axis=1)
            o = jnp.dot(kron, rhs, preferred_element_type=F32).astype(BF16)
            for x in range(nt):
                for z in range(nt):
                    top = (x * nt + z) * 16
                    for r in range(2):
                        row = x * 128 + r * 64 + d * 16
                        mixed[s, row : row + 16, z * 128 : (z + 1) * 128] = o[top : top + 16, r * 128 : (r + 1) * 128]
        return 0

    lax.fori_loop(0, splits, one_split, 0)


def mix(b, weight, rules, mine, theirs, nt):
    return pl.pallas_call(
        functools.partial(mix_kernel, nt, b),
        out_shape=jax.ShapeDtypeStruct((weight.shape[1], nt * 128, nt * 128), BF16),
        in_specs=small(1) + near(9),
        out_specs=near(1)[0],
        compiler_params=room(5),
    )(weight, rules, *mine, *theirs)


def contract_kernel(nt, owners, ids_ref, mixed, p1, p2, p3, own, far, keep_ref, send_ref, acc):
    core = ids_ref[1]

    def product(s):
        if len(owners) == 1:
            mine, at = core == owners[0][2], s
        else:
            mine = core == jnp.where(s < owners[0][1], owners[0][2], owners[1][2])
            skipped = mixed.shape[0] - far.shape[0]
            at = jnp.clip(jnp.where(core == 1, s, s - skipped), 0, far.shape[0] - 1)
        rhs = jnp.concatenate([p1[s], p2[s], p3[s], jnp.where(mine, own[s], far[at])], axis=1)
        rhs = rhs.reshape(nt * 128, rhs.shape[2])
        return jnp.dot(mixed[s], rhs, preferred_element_type=F32).reshape(acc.shape)

    acc[...] = product(0)

    def more(s, _):
        acc[...] += product(s)
        return 0

    last = mixed.shape[0] - 1
    lax.fori_loop(1, last, more, 0)
    total = acc[...] + product(last)
    keep_ref[0] = total[:, :64]
    send_ref[0] = total[:, 64:]


def contract(b, ids, mixed, pieces, own, far, nt):
    cols = own.shape[3]
    out = jax.ShapeDtypeStruct((1, nt, 64, cols), F32)
    return pl.pallas_call(
        functools.partial(contract_kernel, nt, OWNERS[b]),
        out_shape=(out, out),
        in_specs=small(1) + near(6),
        out_specs=tuple(near(2)),
        scratch_shapes=[pltpu.VMEM((nt, 128, cols), F32)],
        compiler_params=room(5),
    )(ids, mixed, *pieces, own, far)


def add_kernel(ids_ref, keep_ref, got_ref, *outs):
    y, x = ids_ref[2], ids_ref[3]
    for d, out in enumerate(outs):
        at = (x + d - y + 4) % 4
        rows = pl.ds(pl.multiple_of(at * 16, 16), 16)
        out[...] = keep_ref[:, :, rows, :] + got_ref[:, :, rows, :]


def add_cores(ids, keep, got):
    size, nt, rows, cols = keep.shape
    return pl.pallas_call(
        add_kernel,
        out_shape=(jax.ShapeDtypeStruct((size, nt, rows // 4, cols), F32),) * 4,
        in_specs=[pl.BlockSpec(memory_space=pltpu.SMEM)] + [pl.BlockSpec(memory_space=pltpu.VMEM)] * 2,
        out_specs=(pl.BlockSpec(memory_space=pltpu.VMEM),) * 4,
        compiler_params=room(3),
    )(ids, keep, got)


def pairs_kernel(nt, splits, ids_ref, pair_ref, rule_ref, high_ref, codes_ref, *outs):
    outs, rules_ref = outs[:-1], outs[-1]
    group = lax.broadcasted_iota(jnp.int32, (1, rules_ref.shape[1]), 1) // 16
    for n in range(nt):
        for m in range(nt):
            line = jnp.full(group.shape, rule_ref[n, 0, m], F32)
            for y in range(1, nt):
                line = jnp.where(group == y, rule_ref[n, y, m], line)
            rules_ref[n * nt + m : n * nt + m + 1, :] = line
    z, core, y, x = ids_ref[0], ids_ref[1], ids_ref[2], ids_ref[3]
    _, _, rows, cols = outs[0].shape
    start = ((z * 2 + core) * 4 + x) * rows
    lane = lax.broadcasted_iota(jnp.int32, (rows, 128), 1)
    sub = lax.broadcasted_iota(jnp.int32, (rows, 128), 0)
    first = y * (cols // 128)
    for b, (out, at) in enumerate((out, at) for out in outs for at in range(out.shape[0])):
        row_block = (ids_ref[4] + b) * 8
        col_block = (ids_ref[4] + b + splits + 1) * 8
        line = codes_ref[pl.ds(row_block + start // 128, 1), :].astype(F32)
        code = jnp.sum(jnp.where(lane == start % 128 + sub, line, 0.0), axis=1, keepdims=True)
        column = jnp.concatenate(
            [codes_ref[pl.ds(col_block + first + n, 1), :] for n in range(cols // 128)], axis=1
        )
        high = high_ref[b]
        for n in range(nt):

            def factor(u):
                t = jnp.where(column == 0, pair_ref[u, 0, n], pair_ref[u, 1, n])
                t = jnp.where(column == 2, pair_ref[u, 2, n], t)
                return jnp.where(column == 3, pair_ref[u, 3, n], t)

            pairing = jnp.where(code == 0.0, factor(0), factor(1))
            pairing = jnp.where(code == 2.0, factor(2), pairing)
            out[at, n] = jnp.where(code == 3.0, factor(3), pairing) + high


def pairs_of(ids, pair, rule, high, codes, splits, nt, rows, cols):
    return pl.pallas_call(
        functools.partial(pairs_kernel, nt, splits),
        out_shape=tuple(jax.ShapeDtypeStruct((len(group), nt, rows, cols), F32) for group in GROUPS)
        + (jax.ShapeDtypeStruct((nt * nt, nt * rows), F32),),
        in_specs=small(4) + near(1),
        out_specs=tuple(near(len(GROUPS) + 1)),
        compiler_params=room(3),
        name="pairs",
    )(ids, pair, rule, high, codes)


def finish_kernel(group, pairing_ref, *refs):
    parts, peaks_ref, out_ref, max_ref = refs[:4], refs[4:-2], refs[-2], refs[-1]
    lane = lax.broadcasted_iota(jnp.int32, (1, 128), 1)
    row = peaks_ref[0][...] if peaks_ref else jnp.full((1, 128), -jnp.inf, F32)
    for at, b in enumerate(group):
        best = None
        for n in range(out_ref.shape[1]):
            total = (parts[0][at, n] + parts[1][at, n]) + (parts[2][at, n] + parts[3][at, n])
            inside = jnp.log(total) + pairing_ref[at, n]
            out_ref[at, n] = inside
            best = inside if best is None else jnp.maximum(best, inside)
        best = jnp.max(best, axis=1, keepdims=True)
        best = jnp.max(best, axis=0, keepdims=True)
        row = jnp.where(lane == b, best, row)
    max_ref[...] = row


def finish(group, pairing, parts, peaks):
    return pl.pallas_call(
        functools.partial(finish_kernel, group),
        out_shape=(jax.ShapeDtypeStruct(pairing.shape, F32), jax.ShapeDtypeStruct((1, 128), F32)),
        in_specs=[pl.BlockSpec(memory_space=pltpu.VMEM)] * (5 + len(peaks)),
        out_specs=(pl.BlockSpec(memory_space=pltpu.VMEM),) * 2,
        compiler_params=room(3),
    )(pairing, *parts, *peaks)


def subtract_kernel(tops_ref, *refs):
    insides, out_ref, scale_ref = refs[:-2], refs[-2], refs[-1]
    top = jnp.max(tops_ref[...], axis=0)
    lane = lax.broadcasted_iota(jnp.int32, top.shape, 1)
    for b, (ref, at) in enumerate((ref, at) for ref in insides for at in range(ref.shape[0])):
        out_ref[b] = ref[at] - top[:, b : b + 1]
        scale_ref[b] = jnp.max(jnp.where(lane == b, top, -jnp.inf))


def subtract(tops, insides):
    return pl.pallas_call(
        subtract_kernel,
        out_shape=(
            jax.ShapeDtypeStruct((len(OWNERS),) + insides[0].shape[1:], F32),
            jax.ShapeDtypeStruct((len(OWNERS),), F32),
        ),
        in_specs=[pl.BlockSpec(memory_space=pltpu.VMEM)] * (1 + len(insides)),
        out_specs=(pl.BlockSpec(memory_space=pltpu.VMEM), pl.BlockSpec(memory_space=pltpu.SMEM)),
        compiler_params=room(3),
        name="subtract",
    )(tops, *insides)


def compute(left_mant, right_mant, left_scale, right_scale, rule_probs, pair_logp, nucleotides, first_block):
    count, splits, nt, rows = left_mant.shape[:4]
    depth, cols = left_mant.shape[5], right_mant.shape[5]
    nz = lax.axis_size("z")
    core = lax.axis_index("core")
    ids = jnp.stack([lax.axis_index("z"), core, lax.axis_index("y"), lax.axis_index("x"), first_block[0]]).astype(
        jnp.int32
    )

    own = right_mant.reshape(count, splits, nt, right_mant.shape[4], cols)
    sibling = lax.ppermute(own, "core", SWAP)

    def by_core(same, other):
        return jnp.concatenate([jnp.where(core == 0, same, other), jnp.where(core == 0, other, same)], axis=-2)

    chip = by_core(own, sibling)
    blocks = [chip[b] for b in range(count)]
    pieces, far = [], []
    for c, owners in enumerate(OWNERS):
        line = [blocks[c]]
        if c == 0:
            same = lax.ppermute(own[0], ZC, ring_pairs(nz))
            line.append(by_core(same, lax.ppermute(own[0], ZC, cross_pairs(nz))))
        for _ in range(len(line), 4):
            line.append(lax.ppermute(line[-1], ZC, ring_pairs(nz)))
        pieces.append(line[1:])
        last, cores = line[-1], tuple(1 - owner for _, _, owner in owners)
        if len(owners) == 2:
            cut = max(owners[0][1], splits - owners[0][1])
            last = jnp.where(core == 0, last[splits - cut :], last[:cut])
        far.append(lax.ppermute(last, ZC, ring_pairs(nz, cores)))

    keep, give = pick(ids, left_mant.reshape(count, splits * nt * rows, depth), nz, nt * rows)
    got = lax.ppermute(give, "core", SWAP)
    up = [lax.ppermute(v, "y", shift(4, 1)) for v in (keep, got)]
    down = [lax.ppermute(v, "y", shift(4, -1)) for v in (keep, got)]
    across = [lax.ppermute(up[0], "y", shift(4, 1)), lax.ppermute(down[1], "y", shift(4, -1))]
    mine = (keep, down[0], across[0], up[0])
    theirs = (got, down[1], across[1], up[1])

    total_scale = left_scale + right_scale
    highest = jnp.max(total_scale, axis=1)
    weight = jnp.exp(total_scale - highest[:, None])
    *pairings, rules = pairs_of(
        ids,
        jnp.transpose(pair_logp, (1, 2, 0)),
        rule_probs,
        highest,
        nucleotides.reshape(-1, 128),
        splits,
        nt,
        rows,
        cols,
    )
    insides, peaks = [], ()
    for g, group in enumerate(GROUPS):
        kept, sent = contract(g, ids, mix(g, weight, rules, mine, theirs, nt), pieces[g], blocks[g], far[g], nt)
        parts = add_cores(ids, kept, lax.ppermute(sent, "core", SWAP))
        sums = [parts[0]] + [lax.ppermute(parts[d], "x", shift(4, d)) for d in (1, 2, 3)]
        inside, peak = finish(group, pairings[g], sums, peaks)
        peaks = (peak,)
        insides.append(inside)
    everyone = ("z", "core", "y", "x")
    tops = jnp.broadcast_to(peaks[0][None], (lax.axis_size(everyone), 1, 128))
    tops = lax.all_to_all(tops, everyone, split_axis=0, concat_axis=0, tiled=True)
    return subtract(tops, insides)


def solution(mesh):
    split = Mesh(
        mesh.devices.reshape(8, 2, mesh.shape["col"], mesh.shape["layer"]),
        ("z", "core", "y", "x"),
    )
    in_specs = (
        P(None, None, None, ("z", "core", "y"), "x", None),
        P(None, None, None, "x", ("z", "core"), "y"),
        P(),
        P(),
        P(),
        P(),
        P(),
        P(),
    )
    out_specs = (P(None, None, ("z", "core", "x"), "y"), P())
    return jax.shard_map(compute, mesh=split, in_specs=in_specs, out_specs=out_specs, check_vma=False)
```
